32 devices in a mesh: blk: 8 (over y, x, core), grp: 4 (over z).
Axes of the slice: x: 2, y: 2, z: 4, core: 2. Of those that a mesh axis runs over, the one named last changes fastest.
Arguments:
- currents: bfloat16 [4, 16, 65536], P('grp', None, 'blk'), may hold values from -6 to 6
- background: float32 [4, 16, 65536], P('grp', None, 'blk'), may hold values from -6 to 6
- green: bfloat16 [4, 512, 8, 128, 128], P('grp', 'blk'), may hold values from -0.1875 to 0.1875
- offsets: int32 [4, 512, 8], P('grp', 'blk'), may hold values from -128 to 128
- station_cells: int32 [2048, 4], P(('blk', 'grp')), may hold values from 0 to 2047, as said below
- station_green: bfloat16 [2048, 4, 128], P(('blk', 'grp')), may hold values from -0.25 to 0.25
- station_background: float32 [16, 2048], P(None, ('blk', 'grp')), may hold values from -6 to 6
Outputs:
- cell_field: float32 [4, 16, 65536], P('grp', None, 'blk')
- station_field: float32 [16, 2048], P(None, ('blk', 'grp'))
The draws below stay inside these ranges and needn't reach their ends.
Inputs may be any that keep to these rules, and one draw needn't show every extreme that they name: `station_cells`: station s lies with device flat index s // 64; its near blocks lie in blocks from (s // 256 - 1) * 64 to (s // 256 + 2) * 64 - 1, taken modulo 512, in any slab.
All inputs are finite; a program needn't handle non-finite values.
Results may differ from the reference program's by a relative error of at most 0.0003.
Values may be sent and summed in bfloat16 or wider, within the bound.
A program may use at most 64 MiB of HBM per device.

```python
import jax
import jax.numpy as jnp
from jax import lax

C = 128
COLS = 16
NB = 64
KNZ = 8
REACH = 2
KS = 4
STA_DEV = 64
SLABS = 4
BLOCKS_SLAB = 512
CELLS_SLAB = 65536
STATIONS = 2048


def draw_station_cells(key, part):
    first_key, second_key = jax.random.split(key, 2)
    station = jnp.arange(STATIONS, dtype=jnp.int32)
    owner_pos = station // (STA_DEV * SLABS)
    shift_by = jax.random.randint(first_key, (STATIONS, KS), 0 - NB, 2 * NB)
    block = (owner_pos[:, None] * NB + shift_by) % BLOCKS_SLAB
    slab = jax.random.randint(second_key, (STATIONS, KS), 0, SLABS)
    return (slab * BLOCKS_SLAB + block).astype(jnp.int32)


def with_ends(result, stream_key, smallest, largest):
    longest = result.shape.index(max(result.shape))
    spots = []
    for shift in (0, 1):
        where = [jax.random.randint(jax.random.fold_in(stream_key, axis), (), 0, length) for axis, length in enumerate(result.shape)]
        where[longest] = (where[longest] + shift) % result.shape[longest]
        spots.append(tuple(where))
    return result.at[spots[0]].set(smallest).at[spots[1]].set(largest)


def levels(own_key, extent, pieces, least, top_value):
    loudness, own = 1.0, jax.random.fold_in(own_key, 6)
    for axis_at, blocks in pieces:
        steps = jnp.exp(jax.random.uniform(jax.random.fold_in(own, axis_at), (blocks,), jnp.float32, least / len(pieces), top_value / len(pieces)))
        loudness = loudness * jnp.repeat(steps, extent[axis_at] // blocks).reshape([-1 if axis == axis_at else 1 for axis in range(len(extent))])
    return loudness


def centred(own_key, extent, deviation, most, shards=(), kind=jnp.bfloat16):
    entries = jax.random.normal(own_key, extent, jnp.float32) * deviation
    if len(shards) > 0:
        entries = levels(own_key, extent, shards, -0.22, 0.18) * entries
    return jnp.clip(entries, min=-most, max=most).astype(kind)


def setup_inputs(seed: int = 0) -> dict:
    streams_of = jax.random.split(jax.random.key(seed), 8)
    currents = centred(streams_of[0], (SLABS, COLS, CELLS_SLAB), 1.0, 6.0, ((0, 4), (2, 8)))
    background = centred(streams_of[1], (SLABS, COLS, CELLS_SLAB), 1.0, 6.0, ((0, 4), (2, 8)), jnp.float32)
    green = centred(streams_of[2], (SLABS, BLOCKS_SLAB, KNZ, C, C), (C * KNZ) ** -0.5, 0.1875, ((0, 4), (1, 8)))
    offsets = with_ends(jax.random.randint(streams_of[3], (SLABS, BLOCKS_SLAB, KNZ), 0 - REACH * NB, REACH * NB + 1), jax.random.fold_in(streams_of[3], 1), 0 - REACH * NB, REACH * NB).astype(jnp.int32)
    station_cells = draw_station_cells(jax.random.fold_in(streams_of[7], 71), 0)
    station_green = centred(streams_of[5], (STATIONS, KS, C), (KS * C) ** -0.5, 0.25, ((0, 32),))
    station_background = centred(streams_of[6], (COLS, STATIONS), 1.0, 6.0, ((1, 32),), jnp.float32)
    return {"currents": currents, "background": background, "green": green, "offsets": offsets, "station_cells": station_cells, "station_green": station_green, "station_background": station_background}


def slab_field(items):
    cur, back, grn, offs = items
    blocks = cur.reshape(COLS, BLOCKS_SLAB, C).astype(jnp.float32)
    source = (jnp.arange(BLOCKS_SLAB, dtype=jnp.int32)[:, None] + offs) % BLOCKS_SLAB
    picked = blocks[:, source, :]
    anomalous = jnp.einsum("bkpq,cbkq->cbp", grn.astype(jnp.float32), picked)
    return back + anomalous.reshape(COLS, BLOCKS_SLAB * C)


def reference(currents, background, green, offsets, station_cells, station_green, station_background):
    cell_field = lax.map(slab_field, (currents, background, green, offsets))
    everything = currents.reshape(SLABS, COLS, BLOCKS_SLAB, C).astype(jnp.float32)
    slab_index = station_cells // BLOCKS_SLAB
    block_index = station_cells % BLOCKS_SLAB
    picked = everything[slab_index, :, block_index, :]
    station_field = station_background + jnp.einsum("skp,skcp->cs", station_green.astype(jnp.float32), picked)
    return cell_field, station_field
```

```python
import functools

import jax
import jax.numpy as jnp
from jax import lax
from jax.experimental import pallas as pl
from jax.experimental.pallas import tpu as pltpu
from jax.sharding import PartitionSpec as P

REACH = 2
CHUNKS = 8
MESH = pl.DeviceIdType.MESH


def kernel(
    n_blk, n_grp, cur, green, source, near_any, cells_vm, sgreen, anom, sta,
    win, gbuf, sgf, masked, near_v, near_s, parts, ret,
    gsem, cell_sem, wsend, wrecv, ssend, srecv, csend, crecv, psend, precv,
):
    here = lax.axis_index("blk")
    grp = lax.axis_index("grp")
    blocks, knz, cells = green.shape[0], green.shape[1], green.shape[2]
    n_cols = cur.shape[0]
    n_sta, near = cells_vm.shape
    slab_blocks = blocks * n_blk
    step = blocks // CHUNKS

    def green_copy(i):
        part = pl.ds(i * step, step)
        return pltpu.make_async_copy(green.at[part], gbuf.at[part], gsem.at[i])

    def slot(i):
        return win.at[pl.ds(i * blocks, blocks)]

    own_near = pltpu.make_async_copy(near_any, near_s.at[grp], cell_sem.at[0])
    own_near.start()

    odd = here % 2
    sib = here + 1 - 2 * odd
    up2, down2 = (here + 2) % n_blk, (here + n_blk - 2) % n_blk
    barrier = pltpu.get_barrier_semaphore()
    for peer in (sib, up2, down2):
        pl.semaphore_signal(barrier, inc=1, device_id=(peer, grp), device_id_type=MESH)
    for d in range(1, n_grp):
        pl.semaphore_signal(barrier, inc=1, device_id=(here, (grp + d) % n_grp), device_id_type=MESH)
    for b in range(blocks):
        win[REACH * blocks + b] = cur[:, b * cells : (b + 1) * cells]
    mine = slot(REACH)
    pl.semaphore_wait(barrier, 3 + n_grp - 1)

    def to_blk(src, dst, peer, i):
        return pltpu.make_async_remote_copy(
            src_ref=src, dst_ref=dst, send_sem=wsend.at[i], recv_sem=wrecv.at[i],
            device_id=(peer, grp), device_id_type=MESH,
        )

    c_up = to_blk(mine, slot(0), up2, 0)
    c_down = to_blk(mine, slot(2 * REACH), down2, 1)
    c_sib = to_blk(mine, slot(1 + 2 * odd), sib, 2)
    c_up.start()
    c_down.start()
    c_sib.start()

    def to_grp(src, dst, d, send, recv):
        return pltpu.make_async_remote_copy(
            src_ref=src, dst_ref=dst, send_sem=send.at[d], recv_sem=recv.at[d],
            device_id=(here, (grp + d) % n_grp), device_id_type=MESH,
        )

    c_cells = [None] + [to_grp(near_any, near_v.at[grp], d, csend, crecv) for d in range(1, n_grp)]
    for d in range(1, n_grp):
        c_cells[d].start()

    sgf[...] = sgreen[...].astype(jnp.float32)
    c_rows = [None]
    for d in list(range(1, n_grp)) + [0]:
        peer = (grp + d) % n_grp
        first = peer * slab_blocks
        for k in range(near):
            at = jnp.broadcast_to(cells_vm[:, k : k + 1], (n_sta, cells))
            rows = sgf[pl.ds(k, n_sta, stride=near), :]
            rows = jnp.where((at >= first) & (at < first + slab_blocks), rows, 0.0)
            masked[d, :, k * cells : (k + 1) * cells] = rows.astype(jnp.bfloat16)
        if d > 0:
            c_rows.append(to_grp(masked.at[d], masked.at[n_grp + d], d, ssend, srecv))
            c_rows[d].start()

    for i in range(CHUNKS):
        green_copy(i).start()

    for d in range(1, n_grp):
        c_cells[d].wait_recv()
    c_own = [None]
    for d in range(1, n_grp):
        src = (grp + n_grp - d) % n_grp
        c_own.append(pltpu.make_async_copy(near_v.at[src], near_s.at[src], cell_sem.at[d]))
        c_own[d].start()

    c_up.wait_recv()
    c_down.wait_recv()
    c_fwd = to_blk(slot(2 * REACH * (1 - odd)), slot(3 - 2 * odd), sib, 3)
    c_fwd.start()
    own_near.wait()
    for d in range(1, n_grp):
        c_own[d].wait()
        c_rows[d].wait_recv()
    c_sib.wait_recv()
    c_fwd.wait_recv()

    group = 8
    c_parts = [None]
    for d in list(range(1, n_grp)) + [0]:
        src = (grp + n_grp - d) % n_grp
        rhs_at = n_grp + d if d > 0 else 0

        def stations(t, acc, src=src, rhs_at=rhs_at):
            rows = []
            for s in range(group):
                row = []
                for k in range(near):
                    row.append(win[near_s[src, t * group + s, k]])
                rows.append(jnp.concatenate(row, axis=1))
            lhs = jnp.concatenate(rows, axis=0)
            full = lax.dot_general(
                lhs, masked[rhs_at], (((1,), (1,)), ((), ())), preferred_element_type=jnp.float32
            )
            lane = lax.broadcasted_iota(jnp.int32, acc.shape, 1)
            for s in range(group):
                part = full[s * n_cols : (s + 1) * n_cols, :]
                acc = acc + jnp.where(lane == t * group + s, part, 0.0)
            return acc

        parts[d] = lax.fori_loop(0, n_sta // group, stations, jnp.zeros(parts.shape[1:], jnp.float32))
        if d > 0:
            copy = pltpu.make_async_remote_copy(
                src_ref=parts.at[d], dst_ref=ret.at[d], send_sem=psend.at[d], recv_sem=precv.at[d],
                device_id=(here, src), device_id_type=MESH,
            )
            copy.start()
            c_parts.append(copy)

    for i in range(CHUNKS):
        green_copy(i).wait()

        def row(t, carry, i=i):
            b = i * step + t
            lhs = jnp.concatenate([win[source[b, k]] for k in range(knz)], axis=1)
            rhs = jnp.concatenate([gbuf[b, k] for k in range(knz)], axis=1)
            anom[:, pl.ds(pl.multiple_of(b * cells, 128), cells)] = lax.dot_general(
                lhs, rhs, (((1,), (1,)), ((), ())), preferred_element_type=jnp.float32
            )
            return carry

        lax.fori_loop(0, step, row, 0, unroll=4)

    total = parts[0]
    for d in range(1, n_grp):
        c_parts[d].wait_recv()
        total = total + ret[d]
    sta[...] = total
    for copy in (c_up, c_down, c_sib, c_fwd):
        copy.wait_send()
    for d in range(1, n_grp):
        c_cells[d].wait_send()
        c_rows[d].wait_send()
        c_parts[d].wait_send()


def body(n_blk, n_grp, currents, background, green, offsets, station_cells, station_green, station_background):
    _, n_cols, span = currents.shape
    _, blocks, knz, cells, _ = green.shape
    n_sta, near = station_cells.shape
    here = lax.axis_index("blk")
    slab_blocks = blocks * n_blk
    source = jnp.arange(blocks, dtype=jnp.int32)[:, None] + offsets[0] + REACH * blocks
    position = (station_cells % slab_blocks - (here - 1) * blocks) % slab_blocks + (REACH - 1) * blocks
    any_spec = pl.BlockSpec(memory_space=pl.ANY)
    vmem = pl.BlockSpec(memory_space=pltpu.VMEM)
    dma = pltpu.SemaphoreType.DMA
    anomalous, extra = pl.pallas_call(
        functools.partial(kernel, n_blk, n_grp),
        out_shape=(
            jax.ShapeDtypeStruct((n_cols, span), jnp.float32),
            jax.ShapeDtypeStruct((n_cols, n_sta), jnp.float32),
        ),
        in_specs=[
            vmem, any_spec, pl.BlockSpec(memory_space=pltpu.SMEM), any_spec, vmem, vmem,
        ],
        out_specs=(vmem, vmem),
        scratch_shapes=[
            pltpu.VMEM(((2 * REACH + 1) * blocks, n_cols, cells), jnp.bfloat16),
            pltpu.VMEM((blocks, knz, cells, cells), jnp.bfloat16),
            pltpu.VMEM((n_sta * near, cells), jnp.float32),
            pltpu.VMEM((2 * n_grp, n_sta, near * cells), jnp.bfloat16),
            pltpu.VMEM((n_grp, n_sta, near), jnp.int32),
            pltpu.SMEM((n_grp, n_sta, near), jnp.int32),
            pltpu.VMEM((n_grp, n_cols, n_sta), jnp.float32),
            pltpu.VMEM((n_grp, n_cols, n_sta), jnp.float32),
            dma((CHUNKS,)), dma((n_grp,)), dma((4,)), dma((4,)),
            dma((n_grp,)), dma((n_grp,)), dma((n_grp,)), dma((n_grp,)), dma((n_grp,)), dma((n_grp,)),
        ],
        compiler_params=pltpu.CompilerParams(
            collective_id=0, has_side_effects=True, vmem_limit_bytes=56 * 1024 * 1024
        ),
    )(
        currents[0], green[0], source, position, station_cells,
        station_green.reshape(n_sta * near, cells),
    )
    return background + anomalous[None], station_background + extra


def solution(mesh):
    return jax.shard_map(
        functools.partial(body, mesh.shape["blk"], mesh.shape["grp"]),
        mesh=mesh,
        in_specs=(
            P("grp", None, "blk"),
            P("grp", None, "blk"),
            P("grp", "blk", None, None, None),
            P("grp", "blk", None),
            P(("blk", "grp"), None),
            P(("blk", "grp"), None, None),
            P(None, ("blk", "grp")),
        ),
        out_specs=(P("grp", None, "blk"), P(None, ("blk", "grp"))),
        check_vma=False,
    )
```

```python
import functools

import jax
import jax.numpy as jnp
from jax import lax
from jax.experimental import pallas as pl
from jax.experimental.pallas import tpu as pltpu
from jax.sharding import PartitionSpec as P

REACH = 2
CHUNKS = 8
PIECES = 8
LANES = 128
MESH = pl.DeviceIdType.MESH


def kernel(
    n_blk, n_grp, cur_in, green, offs_in, cells_in, rows_in, anom, sta,
    win, gbuf, cur, offs, near_cells, rows, rowf, rhs_st, table, source, near_v, near_s, parts, ret,
    gsem, lsem, tsem, nsem, wsend, wrecv, ssend, srecv, csend, crecv, psend, precv,
):
    here = lax.axis_index("blk")
    grp = lax.axis_index("grp")
    blocks, knz, cells = green.shape[0], green.shape[1], green.shape[2]
    n_cols = cur.shape[0]
    near, n_sta = near_cells.shape
    slab_blocks = blocks * n_blk
    step = blocks // CHUNKS
    nothing = (2 * REACH + 1) * blocks

    odd = here % 2
    sib = here + 1 - 2 * odd
    par = here // 2 % 2
    partner = here + 2 - 4 * par
    far = (here + n_blk + 4 - 8 * par) % n_blk
    far_from = (here + n_blk - 4 + 8 * par) % n_blk
    size = blocks // PIECES
    barrier = pltpu.get_barrier_semaphore()
    for peer in (sib, partner, far_from):
        pl.semaphore_signal(barrier, inc=1, device_id=(peer, grp), device_id_type=MESH)
    for d in range(1, n_grp):
        pl.semaphore_signal(barrier, inc=1, device_id=(here, (grp + d) % n_grp), device_id_type=MESH)

    loads = [
        pltpu.make_async_copy(src, dst, lsem.at[i])
        for i, (src, dst) in enumerate(
            ((cur_in, cur), (cells_in, near_cells), (offs_in, offs), (rows_in, rows.at[0]))
        )
    ]
    for load in loads:
        load.start()

    def green_copy(i):
        part = pl.ds(i * step, step)
        return pltpu.make_async_copy(green.at[part], gbuf.at[part], gsem.at[i])

    def slot(i):
        return win.at[pl.ds(i * blocks, blocks)]

    def chunk_of(i, j):
        return win.at[pl.ds(i * blocks + j * size, size)]

    win[nothing] = jnp.zeros((n_cols, cells), jnp.bfloat16)
    table[...] = jnp.zeros(table.shape, jnp.int32)
    near_v[:n_grp] = jnp.zeros((n_grp,) + near_v.shape[1:], jnp.int32)
    loads[1].wait()
    loads[2].wait()
    table[:knz, :blocks] = offs[...] + lax.broadcasted_iota(jnp.int32, (knz, blocks), 1) + REACH * blocks
    to_source = pltpu.make_async_copy(table, source, tsem)
    to_source.start()
    at = near_cells[...]
    rel = at
    for q in range(1, n_grp):
        rel = jnp.where(at >= q * slab_blocks, at - q * slab_blocks, rel)
    rel = rel - (here - 1) * blocks
    rel = jnp.where(rel < 0, rel + slab_blocks, rel)
    rel = jnp.where(rel >= slab_blocks, rel - slab_blocks, rel) + (REACH - 1) * blocks
    for d in range(n_grp):
        first = (grp + d) % n_grp * slab_blocks
        held = (at >= first) & (at < first + slab_blocks)
        near_v[d, :near, :n_sta] = jnp.where(held, jnp.minimum(rel, nothing), nothing)
    loads[0].wait()
    for b in range(blocks):
        win[REACH * blocks + b] = cur[:, b * cells : (b + 1) * cells]
    mine = slot(REACH)
    pl.semaphore_wait(barrier, 3 + n_grp - 1)

    def to_blk(src, dst, peer, i):
        return pltpu.make_async_remote_copy(
            src_ref=src, dst_ref=dst, send_sem=wsend.at[i], recv_sem=wrecv.at[i],
            device_id=(peer, grp), device_id_type=MESH,
        )

    c_sib = to_blk(mine, slot(1 + 2 * odd), sib, 0)
    c_pair = [to_blk(chunk_of(REACH, j), chunk_of(4 * par, j), partner, 1 + j) for j in range(PIECES)]
    for j in range(PIECES):
        c_pair[j].start()

    def to_grp(src, dst, d, send, recv):
        return pltpu.make_async_remote_copy(
            src_ref=src, dst_ref=dst, send_sem=send.at[d], recv_sem=recv.at[d],
            device_id=(here, (grp + d) % n_grp), device_id_type=MESH,
        )

    c_near, c_rows = [None], [None]
    for d in range(1, n_grp):
        c_near.append(to_grp(near_v.at[d], near_v.at[n_grp + d], d, csend, crecv))
        c_near[d].start()
    for d in range(1, n_grp):
        c_rows.append(to_grp(rows_in, rows.at[d], d, ssend, srecv))
        c_rows[d].start()
    c_sib.start()
    for i in range(CHUNKS):
        green_copy(i).start()
    c_far = []
    for j in range(PIECES):
        c_pair[j].wait_recv()
        c_far.append(to_blk(chunk_of(4 - 4 * par, j), chunk_of(4 * par, j), far, 1 + PIECES + j))
        c_far[j].start()

    to_near = [pltpu.make_async_copy(near_v.at[0], near_s.at[0], nsem.at[0])]
    to_near[0].start()
    for d in range(1, n_grp):
        c_near[d].wait_recv()
        to_near.append(pltpu.make_async_copy(near_v.at[n_grp + d], near_s.at[d], nsem.at[d]))
        to_near[d].start()
    loads[3].wait()
    for d in range(n_grp):
        if d > 0:
            c_rows[d].wait_recv()
        rowf[d] = rows[d].astype(jnp.float32)
        for k in range(near):
            piece = rowf[d, pl.ds(k, n_sta, stride=near), :]
            rhs_st[d, :, k * cells : (k + 1) * cells] = piece.astype(jnp.bfloat16)
    to_source.wait()
    for d in range(n_grp):
        to_near[d].wait()

    c_fwd = []
    for j in range(PIECES):
        c_far[j].wait_recv()
        c_fwd.append(to_blk(chunk_of(4 - 4 * odd, j), chunk_of(3 - 2 * odd, j), sib, 1 + 2 * PIECES + j))
        c_fwd[j].start()
    c_sib.wait_recv()
    for j in range(PIECES):
        c_fwd[j].wait_recv()

    group = 8
    c_parts = [None]
    for d in list(range(1, n_grp)) + [0]:
        src = (grp + n_grp - d) % n_grp

        def stations(t, acc, d=d):
            picks = []
            for s in range(group):
                row = [win[near_s[d, k, t * group + s]] for k in range(near)]
                picks.append(jnp.concatenate(row, axis=1))
            lhs = jnp.concatenate(picks, axis=0)
            full = lax.dot_general(
                lhs, rhs_st[d], (((1,), (1,)), ((), ())), preferred_element_type=jnp.float32
            )
            lane = lax.broadcasted_iota(jnp.int32, acc.shape, 1)
            for s in range(group):
                part = full[s * n_cols : (s + 1) * n_cols, :]
                acc = acc + jnp.where(lane == t * group + s, part, 0.0)
            return acc

        parts[d] = lax.fori_loop(
            0, n_sta // group, stations, jnp.zeros(parts.shape[1:], jnp.float32), unroll=8
        )
        if d > 0:
            copy = pltpu.make_async_remote_copy(
                src_ref=parts.at[d], dst_ref=ret.at[d], send_sem=psend.at[d], recv_sem=precv.at[d],
                device_id=(here, src), device_id_type=MESH,
            )
            copy.start()
            c_parts.append(copy)

    for i in range(CHUNKS):
        green_copy(i).wait()

    def row(b, carry):
        lhs = jnp.concatenate([win[source[k, b]] for k in range(knz)], axis=1)
        rhs = jnp.concatenate([gbuf[b, k] for k in range(knz)], axis=1)
        anom[:, pl.ds(pl.multiple_of(b * cells, 128), cells)] = lax.dot_general(
            lhs, rhs, (((1,), (1,)), ((), ())), preferred_element_type=jnp.float32
        )
        return carry

    lax.fori_loop(0, blocks, row, 0, unroll=8)

    total = parts[0]
    for d in range(1, n_grp):
        c_parts[d].wait_recv()
        total = total + ret[d]
    sta[...] = total
    for copy in [c_sib] + c_pair + c_far + c_fwd:
        copy.wait_send()
    for d in range(1, n_grp):
        c_near[d].wait_send()
        c_rows[d].wait_send()
        c_parts[d].wait_send()


def finish(anom, extra, background, station_background, cell_out, sta_out):
    cell_out[...] = background[...] + anom[...]
    sta_out[...] = station_background[...] + extra[...]


def body(n_blk, n_grp, currents, background, green, offsets, station_cells, station_green, station_background):
    _, n_cols, span = currents.shape
    _, blocks, knz, cells, _ = green.shape
    n_sta, near = station_cells.shape
    hbm = pl.BlockSpec(memory_space=pl.ANY)
    vmem = pl.BlockSpec(memory_space=pltpu.VMEM)
    dma = pltpu.SemaphoreType.DMA
    shapes = (
        jax.ShapeDtypeStruct((n_cols, span), jnp.float32),
        jax.ShapeDtypeStruct((n_cols, n_sta), jnp.float32),
    )
    anomalous, extra = pl.pallas_call(
        functools.partial(kernel, n_blk, n_grp),
        out_shape=shapes,
        in_specs=[hbm] * 5,
        out_specs=(vmem, vmem),
        scratch_shapes=[
            pltpu.VMEM(((2 * REACH + 1) * blocks + 1, n_cols, cells), jnp.bfloat16),
            pltpu.VMEM((blocks, knz, cells, cells), jnp.bfloat16),
            pltpu.VMEM((n_cols, span), jnp.bfloat16),
            pltpu.VMEM((knz, blocks), jnp.int32),
            pltpu.VMEM((near, n_sta), jnp.int32),
            pltpu.VMEM((n_grp, n_sta * near, cells), jnp.bfloat16),
            pltpu.VMEM((n_grp, n_sta * near, cells), jnp.float32),
            pltpu.VMEM((n_grp, n_sta, near * cells), jnp.bfloat16),
            pltpu.VMEM((8, LANES), jnp.int32),
            pltpu.SMEM((8, LANES), jnp.int32),
            pltpu.VMEM((2 * n_grp, 8, LANES), jnp.int32),
            pltpu.SMEM((n_grp, 8, LANES), jnp.int32),
            pltpu.VMEM((n_grp, n_cols, n_sta), jnp.float32),
            pltpu.VMEM((n_grp, n_cols, n_sta), jnp.float32),
            dma((CHUNKS,)), dma((4,)), dma(()), dma((n_grp,)), dma((1 + 3 * PIECES,)), dma((1 + 3 * PIECES,)),
            dma((n_grp,)), dma((n_grp,)), dma((n_grp,)), dma((n_grp,)), dma((n_grp,)), dma((n_grp,)),
        ],
        compiler_params=pltpu.CompilerParams(
            collective_id=0, has_side_effects=True, vmem_limit_bytes=56 * 1024 * 1024
        ),
    )(
        currents[0], green[0], offsets[0].T, station_cells.T,
        station_green.reshape(n_sta * near, cells),
    )
    cell_field, station_field = pl.pallas_call(
        finish, out_shape=shapes, in_specs=[vmem] * 4, out_specs=(vmem, vmem)
    )(anomalous, extra, background[0], station_background)
    return cell_field[None], station_field


def solution(mesh):
    return jax.shard_map(
        functools.partial(body, mesh.shape["blk"], mesh.shape["grp"]),
        mesh=mesh,
        in_specs=(
            P("grp", None, "blk"),
            P("grp", None, "blk"),
            P("grp", "blk", None, None, None),
            P("grp", "blk", None),
            P(("blk", "grp"), None),
            P(("blk", "grp"), None, None),
            P(None, ("blk", "grp")),
        ),
        out_specs=(P("grp", None, "blk"), P(None, ("blk", "grp"))),
        check_vma=False,
    )
```
